32 devices in a mesh: groups: 2 (over y), pix: 8 (over z, x), mp: 2 (over core).
Axes of the slice: x: 2, y: 2, z: 4, core: 2. Of those that a mesh axis runs over, the one named last changes fastest.
Arguments:
- cell_vectors: bfloat16 [32768, 512], P(('groups', 'pix')), parts along dimension 0, may hold values from -6 to 6
- summary_vectors: bfloat16 [512, 512], P(('groups', 'pix')), parts along dimension 0, may hold values from -6 to 6
- displacement: int32 [1], replicated, may hold values from 1 to 255
- summary_tile_labels: int32 [256], replicated, may hold values from 0 to 63, as said below
- adjacent_tiles: int32 [64, 8], P('pix'), may hold values from 0 to 63, as said below
- focus_scaling_vector: float32 [512], replicated, may hold values from 0.1 to 1.9
- forward_scaling_vector: float32 [512], replicated, may hold values from 0.1 to 1.9
- asking_lookup_payload_factor: bfloat16 [3, 512, 512], P(None, None, 'mp'), may hold values from -1 to 1
- merging_factor: bfloat16 [512, 512], P('mp'), may hold values from -0.25 to 0.25
- expanding_factor: bfloat16 [512, 1024], P(None, 'mp'), may hold values from -0.25 to 0.25
- contracting_factor: bfloat16 [1024, 512], P('mp'), may hold values from -0.1875 to 0.1875
Outputs:
- cell_vectors_final: bfloat16 [32768, 512], P(('groups', 'pix', 'mp')), parts along dimension 0
- summary_vectors_final: bfloat16 [512, 512], P(('groups', 'pix')), parts along dimension 0
The draws below stay inside these ranges and needn't reach their ends.
There are 2 independent parts, one for each index of `groups`. The reference program is written for one: setup_inputs(seed, part) draws one part's arguments, and reference() takes and returns one part's arrays. A program takes and returns all parts, laid end to end along the dimension named above; an argument that names none is the same for every part. Nothing has to cross between parts.
Inputs may be any that keep to these rules, and one draw needn't show every extreme that they name: `summary_tile_labels`: each window has exactly 4 carriers, and the carriers stored with a device's windows belong to those windows. `adjacent_tiles`: column 0 of row w is (w + 1) mod 64; a row may name a window more than once.
All inputs are finite; a program needn't handle non-finite values.
Results may differ from the reference program's by a relative error of at most 0.013.
Values may be sent and summed in bfloat16 or wider, within the bound.
A program may use at most 64 MiB of HBM per device.

```python
import jax
import jax.numpy as jnp
from jax import lax

NUM_FOCI = 8
SPAN_DIMENSION = 64
EMBED_SIZE = 512
FF = 1024
WIN = 256
SUMMARY_PER_TILE = 4
SEEN_GROUPS = 8
TILES_PER_SHARD = 8
NWIN = 64
PIXELS = 16384
SUMMARY_ALL = 256


def embedding_array(key, count):
    return jnp.clip(jax.random.normal(key, (count, EMBED_SIZE), jnp.float32), -6.0, 6.0)


def draw_cell_vectors(key, part):
    return embedding_array(key, PIXELS).astype(jnp.bfloat16)


def draw_summary_vectors(key, part):
    return embedding_array(key, SUMMARY_ALL).astype(jnp.bfloat16)


def draw_asking_lookup_payload_factor(key, part):
    return (jnp.clip(jax.random.normal(key, (3, EMBED_SIZE, EMBED_SIZE), jnp.float32), -6.0, 6.0) * EMBED_SIZE ** (-0.5)).astype(jnp.bfloat16)


def draw_summary_tile_labels(key, part):
    segment_list = NWIN // TILES_PER_SHARD
    each_segment = SUMMARY_PER_TILE * TILES_PER_SHARD
    raw = jax.random.randint(key, (segment_list, each_segment), 0, 2 ** 20) * each_segment + jnp.arange(each_segment, dtype=jnp.int32)[None, :]
    sorting_permutation = jnp.argsort(raw, axis=1).astype(jnp.int32)
    starting_offset = (jnp.arange(segment_list, dtype=jnp.int32) * TILES_PER_SHARD)[:, None]
    return (starting_offset + sorting_permutation // SUMMARY_PER_TILE).reshape(segment_list * each_segment).astype(jnp.int32)


def draw_adjacent_tiles(key, part):
    window_ids = jnp.arange(NWIN, dtype=jnp.int32)
    first = ((window_ids + 1) % NWIN)[:, None]
    others = jax.random.randint(jax.random.fold_in(key, 7), (NWIN, SEEN_GROUPS - 1), 0, NWIN)
    return jnp.concatenate([first, others], axis=1).astype(jnp.int32)


def block_levels(rng, extent, pieces, least, largest):
    def one(axis_at, shards_of):
        heights = jax.random.uniform(jax.random.fold_in(jax.random.fold_in(rng, 6), axis_at), (shards_of,), jnp.float32, least / len(pieces), largest / len(pieces))
        return jnp.repeat(jnp.exp(heights), extent[axis_at] // shards_of).reshape((-1,) + (1,) * (len(extent) - axis_at - 1))

    factor_of = one(*pieces[0])
    for cut in pieces[1:]:
        factor_of = factor_of * one(*cut)
    return factor_of


def centred(key, extent, scale, limit, cuts=(), kind=jnp.bfloat16):
    drawn = scale * jax.random.normal(key, extent, jnp.float32)
    if cuts:
        drawn = drawn * block_levels(key, extent, cuts, -0.22, 0.18)
    return jnp.clip(drawn, -limit, limit).astype(kind)


def setup_inputs(seed: int = 0, part: int = 0) -> dict:
    keys = jax.random.split(jax.random.key(seed), 12)
    part_splits = jax.random.split(jax.random.fold_in(keys[11], part), 12)
    cell_vectors = draw_cell_vectors(jax.random.fold_in(jax.random.fold_in(keys[11], part), 71), part)
    summary_vectors = draw_summary_vectors(jax.random.fold_in(jax.random.fold_in(keys[11], part), 71), part)
    displacement = jax.random.randint(keys[2], (1,), 1, WIN).astype(jnp.int32)
    summary_tile_labels = draw_summary_tile_labels(jax.random.fold_in(keys[11], 71), part)
    adjacent_tiles = draw_adjacent_tiles(jax.random.fold_in(keys[11], 71), part)
    focus_scaling_vector = jnp.clip(1.0 + 0.18 * jax.random.normal(keys[5], (EMBED_SIZE,), jnp.float32), 0.1, 1.9)
    forward_scaling_vector = jnp.clip(1.0 + 0.18 * jax.random.normal(keys[6], (EMBED_SIZE,), jnp.float32), 0.1, 1.9)
    asking_lookup_payload_factor = draw_asking_lookup_payload_factor(jax.random.fold_in(keys[11], 71), part)
    merging_factor = centred(keys[8], (EMBED_SIZE, EMBED_SIZE), EMBED_SIZE ** -0.5, 0.25, ((0, 2),))
    expanding_factor = centred(keys[9], (EMBED_SIZE, FF), EMBED_SIZE ** -0.5, 0.25, ((1, 2),))
    contracting_factor = centred(keys[10], (FF, EMBED_SIZE), FF ** -0.5, 0.1875, ((0, 2),))
    return dict(cell_vectors=cell_vectors, summary_vectors=summary_vectors, displacement=displacement, summary_tile_labels=summary_tile_labels, adjacent_tiles=adjacent_tiles, focus_scaling_vector=focus_scaling_vector, forward_scaling_vector=forward_scaling_vector, asking_lookup_payload_factor=asking_lookup_payload_factor, merging_factor=merging_factor, expanding_factor=expanding_factor, contracting_factor=contracting_factor)


def quadratic_rescale(values, gain):
    wide = values.astype(jnp.float32)
    scaled = wide * lax.rsqrt(lax.optimization_barrier(jnp.mean(wide * wide, axis=-1, keepdims=True)) + 1e-06)
    return (scaled * gain).astype(jnp.bfloat16)

def reference(cell_vectors, summary_vectors, displacement, summary_tile_labels, adjacent_tiles, focus_scaling_vector, forward_scaling_vector, asking_lookup_payload_factor, merging_factor, expanding_factor, contracting_factor):
    offset = displacement[0]
    normed = quadratic_rescale(cell_vectors, focus_scaling_vector)
    summary_rescaled = quadratic_rescale(summary_vectors, focus_scaling_vector)
    shifted = lax.dynamic_slice_in_dim(jnp.concatenate([normed, normed], 0), offset, PIXELS, 0)

    def linear_map_on(source, index):
        return jnp.dot(source, asking_lookup_payload_factor[index], preferred_element_type=jnp.float32).astype(jnp.bfloat16)
    sharpness_coefficient = SPAN_DIMENSION ** (-0.5)
    queries = linear_map_on(shifted, 0).reshape(NWIN, WIN, NUM_FOCI, SPAN_DIMENSION)
    keys_px = linear_map_on(shifted, 1).reshape(NWIN, WIN, NUM_FOCI, SPAN_DIMENSION)
    values_px = linear_map_on(shifted, 2).reshape(NWIN, WIN, NUM_FOCI, SPAN_DIMENSION)
    digest_question_arrows = linear_map_on(summary_rescaled, 0).reshape(SUMMARY_ALL, NUM_FOCI, SPAN_DIMENSION).astype(jnp.float32)
    digest_probe_arrows = linear_map_on(summary_rescaled, 1).reshape(SUMMARY_ALL, NUM_FOCI, SPAN_DIMENSION).astype(jnp.float32)
    summary_payload_vectors = linear_map_on(summary_rescaled, 2).reshape(SUMMARY_ALL, NUM_FOCI, SPAN_DIMENSION).astype(jnp.float32)

    def one_window(items):
        question_coefficient, probe_weighting, payload_factor, neighbour_vectors = items
        seen_filter = jnp.any(neighbour_vectors[:, None] == summary_tile_labels[None, :], axis=0)
        native = jnp.einsum('eyr,wyr->yew', question_coefficient.astype(jnp.float32), probe_weighting.astype(jnp.float32)) * sharpness_coefficient
        remote_portion = jnp.einsum('eyr,wyr->yew', question_coefficient.astype(jnp.float32), digest_probe_arrows) * sharpness_coefficient
        remote_portion = jnp.where(seen_filter[None, None, :], remote_portion, -jnp.inf)
        scores = jnp.concatenate([native, remote_portion], axis=2)
        top = lax.optimization_barrier(jnp.max(scores, axis=2, keepdims=True))
        weights = jnp.exp(scores - top)
        weights = weights / lax.optimization_barrier(jnp.sum(weights, axis=2, keepdims=True))
        every_payload = jnp.concatenate([payload_factor.astype(jnp.float32), summary_payload_vectors], axis=0)
        result = jnp.einsum('smo,ose->mse', weights, every_payload)
        return result.reshape(WIN, EMBED_SIZE).astype(jnp.bfloat16)
    window_out = lax.map(one_window, (queries, keys_px, values_px, adjacent_tiles)).reshape(PIXELS, EMBED_SIZE)
    digest_raw_scores = jnp.einsum('eyr,wyr->yew', digest_question_arrows, digest_probe_arrows) * sharpness_coefficient
    summary_maximum = lax.optimization_barrier(jnp.max(digest_raw_scores, axis=2, keepdims=True))
    summary_softmax_share = jnp.exp(digest_raw_scores - summary_maximum)
    summary_softmax_share = summary_softmax_share / lax.optimization_barrier(jnp.sum(summary_softmax_share, axis=2, keepdims=True))
    summary_outcome = jnp.einsum('smo,ose->mse', summary_softmax_share, summary_payload_vectors).reshape(SUMMARY_ALL, EMBED_SIZE).astype(jnp.bfloat16)
    restored = lax.dynamic_slice_in_dim(jnp.concatenate([window_out, window_out], 0), PIXELS - offset, PIXELS, 0)
    hidden_state = (cell_vectors.astype(jnp.float32) + jnp.dot(restored, merging_factor, preferred_element_type=jnp.float32)).astype(jnp.bfloat16)
    summary_hidden_state = (summary_vectors.astype(jnp.float32) + jnp.dot(summary_outcome, merging_factor, preferred_element_type=jnp.float32)).astype(jnp.bfloat16)

    def forward_hidden(source):
        normed_two = quadratic_rescale(source, forward_scaling_vector)
        hidden = jax.nn.gelu(jnp.dot(normed_two, expanding_factor, preferred_element_type=jnp.float32), approximate=True).astype(jnp.bfloat16)
        return (source.astype(jnp.float32) + jnp.dot(hidden, contracting_factor, preferred_element_type=jnp.float32)).astype(jnp.bfloat16)
    return (forward_hidden(hidden_state), forward_hidden(summary_hidden_state))
```

```python
import functools

import jax
import jax.numpy as jnp
from jax import lax
from jax.experimental import pallas as pl
from jax.experimental.pallas import tpu as pltpu
from jax.sharding import PartitionSpec as P

HEAD = 64
WIN = 256
PER_TILE = 4
SEEN = 8
SLOTS = PER_TILE * SEEN
SEGMENT = 32
F32 = jnp.float32
BF16 = jnp.bfloat16
NT = (((1,), (1,)), ((), ()))


def rms(values, gain):
    wide = values.astype(F32)
    return wide * lax.rsqrt(jnp.mean(wide * wide, axis=-1, keepdims=True) + 1e-06) * gain


def mm(a, b):
    return jnp.dot(a, b, preferred_element_type=F32)


def mm_nt(a, b):
    return lax.dot_general(a, b, NT, preferred_element_type=F32)


def gelu(x):
    inner = x * (0.7978845608028654 + 0.035677408136300125 * (x * x))
    return 0.5 * x * (1.0 + jnp.tanh(inner))


def kernel(
    n,
    x_hbm,
    c_hbm,
    disp,
    labels,
    adj,
    gain1,
    gain2,
    wqkv_hbm,
    wm_hbm,
    we_hbm,
    wc_hbm,
    out_hbm,
    outc,
    xbuf,
    nrm,
    qkv,
    cbuf,
    kvc,
    qc,
    sel,
    seen,
    wout,
    obuf,
    wqkv,
    wm,
    we,
    wc,
    loc_sem,
    sib_send,
    sib_recv,
    xs_sem,
    xr_sem,
    cs_sem,
    cr_sem,
    os_sem,
    or_sem,
    out_sem,
):
    p = lax.axis_index("pix")
    m = lax.axis_index("mp")
    rows = xbuf.shape[0] - WIN
    tiles = rows // WIN
    total_c = cbuf.shape[0]
    own_c = c_hbm.shape[0]
    nxt = lax.rem(p + 1, n)
    prv = lax.rem(p + n - 1, n)
    sib = {"mp": 1 - m}
    far_pix = lax.rem(p + m, n)
    from_pix = lax.rem(p + m + n - 1, n)
    s = disp[0]

    barrier = pltpu.get_barrier_semaphore()

    def greet(k, _):
        pl.semaphore_signal(
            barrier, inc=1, device_id={"pix": lax.rem(p + k, n)}, device_id_type=pl.DeviceIdType.MESH
        )
        return 0

    lax.fori_loop(1, n, greet, 0)
    pl.semaphore_signal(barrier, inc=1, device_id=sib, device_id_type=pl.DeviceIdType.MESH)
    pl.semaphore_signal(
        barrier,
        inc=1,
        device_id={"pix": from_pix, "mp": 1 - m},
        device_id_type=pl.DeviceIdType.MESH,
    )

    local = [
        pltpu.make_async_copy(
            x_hbm.at[pl.ds(m * rows, rows)], xbuf.at[pl.ds(0, rows)], loc_sem.at[0]
        ),
        pltpu.make_async_copy(c_hbm, cbuf.at[pl.ds(p * own_c, own_c)], loc_sem.at[1]),
        pltpu.make_async_copy(wqkv_hbm, wqkv.at[m], loc_sem.at[2]),
        pltpu.make_async_copy(wm_hbm, wm.at[m], loc_sem.at[3]),
        pltpu.make_async_copy(we_hbm, we.at[m], loc_sem.at[4]),
        pltpu.make_async_copy(wc_hbm, wc.at[m], loc_sem.at[5]),
    ]
    x_copy, c_copy, wqkv_copy, wm_copy, we_copy, wc_copy = local
    x_copy.start()
    wqkv_copy.start()
    c_copy.start()
    wm_copy.start()
    we_copy.start()
    wc_copy.start()
    halo_local = pltpu.make_async_copy(
        x_hbm.at[pl.ds(rows, WIN)], xbuf.at[pl.ds(rows, WIN)], loc_sem.at[6]
    )

    @pl.when(m == 0)
    def _():
        halo_local.start()

    pl.semaphore_wait(barrier, n + 1)

    def to_sibling(src, dst, i):
        return pltpu.make_async_remote_copy(
            src_ref=src,
            dst_ref=dst.at[m],
            send_sem=sib_send.at[i],
            recv_sem=sib_recv.at[i],
            device_id=sib,
            device_id_type=pl.DeviceIdType.MESH,
        )

    halo_remote = pltpu.make_async_remote_copy(
        src_ref=x_hbm.at[pl.ds(0, WIN)],
        dst_ref=xbuf.at[pl.ds(rows, WIN)],
        send_sem=xs_sem,
        recv_sem=xr_sem,
        device_id={"pix": prv},
        device_id_type=pl.DeviceIdType.MESH,
    )
    sends = [
        to_sibling(wqkv_hbm, wqkv, 0),
        to_sibling(wm_hbm, wm, 1),
        to_sibling(we_hbm, we, 2),
        to_sibling(wc_hbm, wc, 3),
    ]

    @pl.when(m == 1)
    def _():
        halo_remote.start()

    sends[0].start()

    def carrier_copy(to, slot):
        return pltpu.make_async_remote_copy(
            src_ref=c_hbm,
            dst_ref=cbuf.at[pl.ds(slot * own_c, own_c)],
            send_sem=cs_sem.at[to],
            recv_sem=cr_sem.at[slot],
            device_id={"pix": to},
            device_id_type=pl.DeviceIdType.MESH,
        )

    def send_carriers(k, _):
        carrier_copy(lax.rem(p + k, n), p).start()
        return 0

    lax.fori_loop(1, n, send_carriers, 0)
    sends[1].start()
    sends[2].start()
    sends[3].start()

    lab = jnp.broadcast_to(labels[...], (8, total_c))
    lane = lax.broadcasted_iota(jnp.int32, (8, total_c), 1)
    within = lax.rem(lane, SEGMENT)
    ordinal = jnp.zeros_like(lab)
    for d in range(1, SEGMENT):
        same = (pltpu.roll(lab, d, 1) == lab) & (within >= d)
        ordinal = ordinal + jnp.where(same, 1, 0)
    place = lab * PER_TILE + ordinal
    row = lax.broadcasted_iota(jnp.int32, (tiles * SLOTS, 128), 0)
    target = jnp.zeros((tiles * SLOTS, 128), jnp.int32)
    for w in range(tiles):
        for c in range(SEEN):
            target = jnp.where(
                row // PER_TILE == w * SEEN + c, adj[m * tiles + w, c] * PER_TILE, target
            )
    target = target + lax.rem(row, PER_TILE)
    for j in range(total_c // 128):
        here = jnp.broadcast_to(place[0:1, j * 128 : (j + 1) * 128], target.shape)
        sel[:, j * 128 : (j + 1) * 128] = jnp.where(here == target, 1.0, 0.0).astype(BF16)

    g1 = gain1[...]
    x_copy.wait()

    def norm_block(b, _):
        at = pl.ds(pl.multiple_of(b * WIN, WIN), WIN)
        nrm[at, :] = rms(xbuf[at, :], g1).astype(BF16)
        return 0

    lax.fori_loop(0, tiles, norm_block, 0)

    i_row = lax.broadcasted_iota(jnp.int32, (WIN, 2 * WIN), 0)
    i_col = lax.broadcasted_iota(jnp.int32, (WIN, 2 * WIN), 1)
    ahead = jnp.where(i_col == i_row + s, 1.0, 0.0).astype(BF16)
    back = jnp.where(i_col == i_row + (WIN - s), 1.0, 0.0).astype(BF16)

    wqkv_copy.wait()

    def project(w, g):
        at = pl.ds(pl.multiple_of(w * WIN, WIN), 2 * WIN)
        rows_w = mm(ahead, nrm[at, :]).astype(BF16)
        qkv[0, g, w] = (mm(rows_w, wqkv[g, 0]).astype(BF16) * 0.125).astype(BF16)
        qkv[1, g, w] = mm(rows_w, wqkv[g, 1]).astype(BF16)
        qkv[2, g, w] = mm(rows_w, wqkv[g, 2]).astype(BF16)

    def project_own(w, _):
        project(w, m)
        return 0

    lax.fori_loop(0, tiles - 1, project_own, 0)

    @pl.when(m == 0)
    def _():
        halo_local.wait()

    @pl.when(m == 1)
    def _():
        halo_remote.wait_recv()

    nrm[pl.ds(rows, WIN), :] = rms(xbuf[pl.ds(rows, WIN), :], g1).astype(BF16)
    project(tiles - 1, m)
    sends[0].wait_recv()

    def project_far(w, _):
        project(w, 1 - m)
        return 0

    lax.fori_loop(0, tiles, project_far, 0)

    c_copy.wait()

    def wait_carriers(k, _):
        carrier_copy(p, lax.rem(p + k, n)).wait_recv()
        return 0

    lax.fori_loop(1, n, wait_carriers, 0)
    own_rows = rms(cbuf[pl.ds(pl.multiple_of(p * own_c, own_c), own_c), :], g1).astype(BF16)
    for g in range(2):
        qc[g] = (mm(own_rows, wqkv[g, 0]).astype(BF16) * 0.125).astype(BF16)

    def carrier_block(b, _):
        at = pl.ds(pl.multiple_of(b * WIN, WIN), WIN)
        rows_c = rms(cbuf[at, :], g1).astype(BF16)
        for g in range(2):
            for t in range(2):
                kvc[t, g, at, :] = mm(rows_c, wqkv[g, t + 1]).astype(BF16)
        return 0

    lax.fori_loop(0, total_c // WIN, carrier_block, 0)
    for t in range(2):
        for g in range(2):
            picked = mm(sel[...], kvc[t, g]).astype(BF16)
            for w in range(tiles):
                seen[t, g, w] = picked[w * SLOTS : (w + 1) * SLOTS]

    head_lane = lax.broadcasted_iota(jnp.int32, (1, 256), 1) // HEAD
    head_masks = [jnp.where(head_lane == h, 1.0, 0.0).astype(BF16) for h in range(4)]
    brow = lax.broadcasted_iota(jnp.int32, (128, 256), 0) // SLOTS
    bcol = lax.broadcasted_iota(jnp.int32, (128, 256), 1) // HEAD
    block_mask = jnp.where(brow == bcol, 1.0, 0.0).astype(BF16)
    slot_lane = lax.broadcasted_iota(jnp.int32, (1, 128), 1)
    slot_head = slot_lane // SLOTS
    slot_group = lax.rem(slot_lane, SLOTS) // PER_TILE

    def attend(w):
        bias = jnp.zeros((1, 128), F32)
        for c in range(1, SEEN):
            double = jnp.float32(0.0)
            for c2 in range(c):
                double = jnp.where(
                    adj[m * tiles + w, c] == adj[m * tiles + w, c2], jnp.float32(-1e30), double
                )
            bias = jnp.where(slot_group == c, double, bias)
        for g in range(2):
            q = qkv[0, g, w]
            k = qkv[1, g, w]
            v = qkv[2, g, w]
            ks = jnp.concatenate([seen[0, g, w]] * 4, axis=0) * block_mask
            vs = jnp.concatenate([seen[1, g, w]] * 4, axis=0) * block_mask
            s_seen = mm_nt(q, ks) + bias
            top_seen = jnp.zeros((WIN, 128), F32)
            summed = jnp.zeros((WIN, 256), F32)
            total = jnp.zeros((WIN, 256), F32)
            for h in range(4):
                sc = mm_nt(q * head_masks[h], k)
                both = jnp.maximum(
                    jnp.maximum(sc[:, :128], sc[:, 128:]),
                    jnp.where(slot_head == h, s_seen, -jnp.inf),
                )
                top = jnp.max(both, axis=1, keepdims=True)
                pr = jnp.exp(sc - top).astype(BF16)
                top_seen = jnp.where(slot_head == h, top, top_seen)
                summed += mm(pr, v * head_masks[h])
                total += mm(pr, jnp.broadcast_to(head_masks[h], (WIN, 256)))
            ps = jnp.exp(s_seen - top_seen).astype(BF16)
            summed += mm(ps, vs)
            total += mm(ps, block_mask)
            got = (summed / total).astype(BF16)
            wout[pl.ds(pl.multiple_of((w + 1) * WIN, WIN), WIN), g * 256 : (g + 1) * 256] = got

    attend(tiles - 1)
    out_halo = pltpu.make_async_remote_copy(
        src_ref=wout.at[pl.ds(tiles * WIN, WIN)],
        dst_ref=wout.at[pl.ds(0, WIN)],
        send_sem=os_sem,
        recv_sem=or_sem,
        device_id={"pix": far_pix, "mp": 1 - m},
        device_id_type=pl.DeviceIdType.MESH,
    )
    out_halo.start()

    def attend_one(w, _):
        attend(w)
        return 0

    lax.fori_loop(0, tiles - 1, attend_one, 0)

    wm_copy.wait()
    we_copy.wait()
    wc_copy.wait()
    sends[1].wait_recv()
    sends[2].wait_recv()
    sends[3].wait_recv()
    g2 = gain2[...]

    def finish(source, pulled):
        mid = (source.astype(F32) + (mm(pulled[:, :256], wm[0]) + mm(pulled[:, 256:], wm[1]))).astype(
            BF16
        )
        n2 = rms(mid, g2).astype(BF16)
        h0 = gelu(mm(n2, we[0])).astype(BF16)
        h1 = gelu(mm(n2, we[1])).astype(BF16)
        return (mid.astype(F32) + (mm(h0, wc[0]) + mm(h1, wc[1]))).astype(BF16)

    def out_copy(b):
        at = pl.ds(pl.multiple_of(b * WIN, WIN), WIN)
        return pltpu.make_async_copy(obuf.at[at], out_hbm.at[at], out_sem.at[b])

    def finish_block(b):
        at = pl.ds(pl.multiple_of(b * WIN, WIN), WIN)
        pulled = mm(back, wout[pl.ds(pl.multiple_of(b * WIN, WIN), 2 * WIN), :]).astype(BF16)
        obuf[at, :] = finish(xbuf[at, :], pulled)
        out_copy(b).start()

    def finish_one(b, _):
        finish_block(b)
        return 0

    lax.fori_loop(1, tiles, finish_one, 0)

    parts = []
    for g in range(2):
        qs = jnp.concatenate([qc[g]] * 4, axis=0) * block_mask
        sc = mm_nt(qs, kvc[0, g])
        pr = jnp.exp(sc - jnp.max(sc, axis=1, keepdims=True))
        low = pr.astype(BF16)
        res = mm(low, kvc[1, g]) / jnp.sum(pr, axis=1, keepdims=True)
        res = jnp.where(brow == bcol, res, 0.0)
        parts.append(res[0:32] + res[32:64] + res[64:96] + res[96:128])
    pulled_c = jnp.concatenate(parts, axis=1).astype(BF16)
    outc[...] = finish(cbuf[pl.ds(pl.multiple_of(p * own_c, own_c), own_c), :], pulled_c)

    out_halo.wait()
    finish_block(0)

    def out_wait(b, _):
        out_copy(b).wait()
        return 0

    lax.fori_loop(0, tiles, out_wait, 0)

    for i in range(4):
        sends[i].wait_send()

    def sent_carriers(k, _):
        carrier_copy(lax.rem(p + k, n), p).wait_send()
        return 0

    lax.fori_loop(1, n, sent_carriers, 0)

    @pl.when(m == 1)
    def _():
        halo_remote.wait_send()


def body(x, c, disp, labels, adj, gain1, gain2, wqkv, wm, we, wc):
    n = lax.axis_size("pix")
    rows = x.shape[0] // lax.axis_size("mp")
    tiles = rows // WIN
    width = x.shape[1]
    total_c = labels.shape[0]
    own_c = c.shape[0]
    vm = pl.BlockSpec(memory_space=pltpu.VMEM)
    sm = pl.BlockSpec(memory_space=pltpu.SMEM)
    hb = pl.BlockSpec(memory_space=pl.ANY)
    dma = pltpu.SemaphoreType.DMA
    return pl.pallas_call(
        functools.partial(kernel, n),
        out_shape=(
            jax.ShapeDtypeStruct((rows, width), BF16),
            jax.ShapeDtypeStruct((own_c, width), BF16),
        ),
        in_specs=[hb, hb, sm, vm, sm, vm, vm, hb, hb, hb, hb],
        out_specs=(hb, vm),
        scratch_shapes=[
            pltpu.VMEM((rows + WIN, width), BF16),
            pltpu.VMEM((rows + WIN, width), BF16),
            pltpu.VMEM((3, 2, tiles, WIN, 256), BF16),
            pltpu.VMEM((total_c, width), BF16),
            pltpu.VMEM((2, 2, total_c, 256), BF16),
            pltpu.VMEM((2, own_c, 256), BF16),
            pltpu.VMEM((tiles * SLOTS, total_c), BF16),
            pltpu.VMEM((2, 2, tiles, SLOTS, 256), BF16),
            pltpu.VMEM((rows + WIN, width), BF16),
            pltpu.VMEM((rows, width), BF16),
            pltpu.VMEM((2,) + wqkv.shape, BF16),
            pltpu.VMEM((2,) + wm.shape, BF16),
            pltpu.VMEM((2,) + we.shape, BF16),
            pltpu.VMEM((2,) + wc.shape, BF16),
            dma((7,)),
            dma((4,)),
            dma((4,)),
            dma,
            dma,
            dma((n,)),
            dma((n,)),
            dma,
            dma,
            dma((tiles,)),
        ],
        compiler_params=pltpu.CompilerParams(
            collective_id=0, has_side_effects=True, vmem_limit_bytes=58 * 1024 * 1024
        ),
    )(
        x,
        c,
        disp,
        labels.reshape(1, -1),
        adj,
        gain1.reshape(1, -1),
        gain2.reshape(1, -1),
        wqkv,
        wm,
        we,
        wc,
    )


def solution(mesh):
    return jax.shard_map(
        body,
        mesh=mesh,
        in_specs=(
            P(("groups", "pix"), None),
            P(("groups", "pix"), None),
            P(),
            P(),
            P("pix", None),
            P(),
            P(),
            P(None, None, "mp"),
            P("mp", None),
            P(None, "mp"),
            P("mp", None),
        ),
        out_specs=(P(("groups", "pix", "mp"), None), P(("groups", "pix"), None)),
        check_vma=False,
    )
```

```python
import functools

import jax
import jax.numpy as jnp
from jax import lax
from jax.experimental import pallas as pl
from jax.experimental.pallas import tpu as pltpu
from jax.sharding import PartitionSpec as P

HEAD = 64
WIN = 256
PER_TILE = 4
SEEN = 8
SLOTS = PER_TILE * SEEN
SEGMENT = 32
F32 = jnp.float32
BF16 = jnp.bfloat16
NT = (((1,), (1,)), ((), ()))


def rms(values, gain):
    wide = values.astype(F32)
    return wide * lax.rsqrt(jnp.mean(wide * wide, axis=-1, keepdims=True) + 1e-06) * gain


def mm(a, b):
    return jnp.dot(a, b, preferred_element_type=F32)


def mm_nt(a, b):
    return lax.dot_general(a, b, NT, preferred_element_type=F32)


def gelu(x):
    inner = x * (0.7978845608028654 + 0.035677408136300125 * (x * x))
    return 0.5 * x * (1.0 + jnp.tanh(inner))


def kernel(
    n,
    x_hbm,
    c_hbm,
    disp,
    labels,
    adj,
    gain1,
    gain2,
    wqkv_hbm,
    wm_hbm,
    we_hbm,
    wc_hbm,
    out_hbm,
    outc,
    xbuf,
    nrm,
    qkv,
    shf,
    pull,
    cbuf,
    kvc,
    qc,
    sel,
    seen,
    wout,
    obuf,
    wqkv,
    wm,
    we,
    wc,
    loc_sem,
    sib_send,
    sib_recv,
    xs_sem,
    xr_sem,
    cs_sem,
    cr_sem,
    os_sem,
    or_sem,
    out_sem,
):
    p = lax.axis_index("pix")
    m = lax.axis_index("mp")
    rows = xbuf.shape[0] - WIN
    tiles = rows // WIN
    total_c = cbuf.shape[0]
    own_c = c_hbm.shape[0]
    nxt = lax.rem(p + 1, n)
    prv = lax.rem(p + n - 1, n)
    sib = {"mp": 1 - m}
    far_pix = lax.rem(p + m, n)
    from_pix = lax.rem(p + m + n - 1, n)
    s = disp[0]

    barrier = pltpu.get_barrier_semaphore()

    def greet(k, _):
        pl.semaphore_signal(
            barrier, inc=1, device_id={"pix": lax.rem(p + k, n)}, device_id_type=pl.DeviceIdType.MESH
        )
        return 0

    lax.fori_loop(1, n, greet, 0)
    pl.semaphore_signal(barrier, inc=1, device_id=sib, device_id_type=pl.DeviceIdType.MESH)
    pl.semaphore_signal(
        barrier,
        inc=1,
        device_id={"pix": from_pix, "mp": 1 - m},
        device_id_type=pl.DeviceIdType.MESH,
    )

    local = [
        pltpu.make_async_copy(
            x_hbm.at[pl.ds(m * rows, rows)], xbuf.at[pl.ds(0, rows)], loc_sem.at[0]
        ),
        pltpu.make_async_copy(c_hbm, cbuf.at[pl.ds(p * own_c, own_c)], loc_sem.at[1]),
        pltpu.make_async_copy(wqkv_hbm, wqkv.at[m], loc_sem.at[2]),
        pltpu.make_async_copy(wm_hbm, wm.at[m], loc_sem.at[3]),
        pltpu.make_async_copy(we_hbm, we.at[m], loc_sem.at[4]),
        pltpu.make_async_copy(wc_hbm, wc.at[m], loc_sem.at[5]),
    ]
    x_copy, c_copy, wqkv_copy, wm_copy, we_copy, wc_copy = local
    x_copy.start()
    wqkv_copy.start()
    c_copy.start()
    wm_copy.start()
    we_copy.start()
    wc_copy.start()
    halo_local = pltpu.make_async_copy(
        x_hbm.at[pl.ds(rows, WIN)], xbuf.at[pl.ds(rows, WIN)], loc_sem.at[6]
    )

    @pl.when(m == 0)
    def _():
        halo_local.start()

    lab = jnp.broadcast_to(labels[...], (8, total_c))
    lane = lax.broadcasted_iota(jnp.int32, (8, total_c), 1)
    within = lax.rem(lane, SEGMENT)
    ordinal = jnp.zeros_like(lab)
    for d in range(1, SEGMENT):
        same = (pltpu.roll(lab, d, 1) == lab) & (within >= d)
        ordinal = ordinal + jnp.where(same, 1, 0)
    place = lab * PER_TILE + ordinal
    row = lax.broadcasted_iota(jnp.int32, (tiles * SLOTS, 128), 0)
    target = jnp.zeros((tiles * SLOTS, 128), jnp.int32)
    for w in range(tiles):
        for c in range(SEEN):
            target = jnp.where(
                row // PER_TILE == w * SEEN + c, adj[m * tiles + w, c] * PER_TILE, target
            )
    target = target + lax.rem(row, PER_TILE)
    for j in range(total_c // 128):
        here = jnp.broadcast_to(place[0:1, j * 128 : (j + 1) * 128], target.shape)
        sel[:, j * 128 : (j + 1) * 128] = jnp.where(here == target, 1.0, 0.0).astype(BF16)

    g1 = gain1[...]
    x_copy.wait()

    def norm_block(b, _):
        at = pl.ds(pl.multiple_of(b * WIN, WIN), WIN)
        nrm[at, :] = rms(xbuf[at, :], g1).astype(BF16)
        return 0

    lax.fori_loop(0, tiles, norm_block, 0)

    pl.semaphore_wait(barrier, n + 1)

    def to_sibling(src, dst, i):
        return pltpu.make_async_remote_copy(
            src_ref=src,
            dst_ref=dst.at[m],
            send_sem=sib_send.at[i],
            recv_sem=sib_recv.at[i],
            device_id=sib,
            device_id_type=pl.DeviceIdType.MESH,
        )

    halo_remote = pltpu.make_async_remote_copy(
        src_ref=x_hbm.at[pl.ds(0, WIN)],
        dst_ref=xbuf.at[pl.ds(rows, WIN)],
        send_sem=xs_sem,
        recv_sem=xr_sem,
        device_id={"pix": prv},
        device_id_type=pl.DeviceIdType.MESH,
    )
    sends = [
        to_sibling(wqkv_hbm, wqkv, 0),
        to_sibling(wm_hbm, wm, 1),
        to_sibling(we_hbm, we, 2),
        to_sibling(wc_hbm, wc, 3),
    ]

    @pl.when(m == 1)
    def _():
        halo_remote.start()

    sends[0].start()

    def carrier_copy(to, slot):
        return pltpu.make_async_remote_copy(
            src_ref=c_hbm,
            dst_ref=cbuf.at[pl.ds(slot * own_c, own_c)],
            send_sem=cs_sem.at[to],
            recv_sem=cr_sem.at[slot],
            device_id={"pix": to},
            device_id_type=pl.DeviceIdType.MESH,
        )

    def send_carriers(k, _):
        carrier_copy(lax.rem(p + k, n), p).start()
        return 0

    lax.fori_loop(1, n, send_carriers, 0)
    sends[1].start()
    sends[2].start()
    sends[3].start()


    i_row = lax.broadcasted_iota(jnp.int32, (WIN, 2 * WIN), 0)
    i_col = lax.broadcasted_iota(jnp.int32, (WIN, 2 * WIN), 1)
    ahead = jnp.where(i_col == i_row + s, 1.0, 0.0).astype(BF16)
    back = jnp.where(i_col == i_row + (WIN - s), 1.0, 0.0).astype(BF16)

    def shift(w):
        at = pl.ds(pl.multiple_of(w * WIN, WIN), 2 * WIN)
        shf[pl.ds(pl.multiple_of(w * WIN, WIN), WIN), :] = mm(ahead, nrm[at, :]).astype(BF16)

    def shift_one(w, _):
        shift(w)
        return 0

    lax.fori_loop(0, tiles - 1, shift_one, 0)
    wqkv_copy.wait()

    def project(lo, hi, g):
        rows_w = shf[lo * WIN : hi * WIN, :]
        for t in range(3):
            got = mm(rows_w, wqkv[g, t]).astype(BF16)
            if t == 0:
                got = (got * 0.125).astype(BF16)
            qkv[t, g, lo * WIN : hi * WIN] = got

    project(0, tiles - 1, m)

    @pl.when(m == 0)
    def _():
        halo_local.wait()

    @pl.when(m == 1)
    def _():
        halo_remote.wait_recv()

    nrm[pl.ds(rows, WIN), :] = rms(xbuf[pl.ds(rows, WIN), :], g1).astype(BF16)
    shift(tiles - 1)
    project(tiles - 1, tiles, m)
    sends[0].wait_recv()
    project(0, tiles, 1 - m)

    c_copy.wait()

    def wait_carriers(k, _):
        carrier_copy(p, lax.rem(p + k, n)).wait_recv()
        return 0

    lax.fori_loop(1, n, wait_carriers, 0)
    own_rows = rms(cbuf[pl.ds(pl.multiple_of(p * own_c, own_c), own_c), :], g1).astype(BF16)
    for g in range(2):
        qc[g] = (mm(own_rows, wqkv[g, 0]).astype(BF16) * 0.125).astype(BF16)

    def carrier_block(b, _):
        at = pl.ds(pl.multiple_of(b * WIN, WIN), WIN)
        rows_c = rms(cbuf[at, :], g1).astype(BF16)
        for g in range(2):
            for t in range(2):
                kvc[t, g, at, :] = mm(rows_c, wqkv[g, t + 1]).astype(BF16)
        return 0

    lax.fori_loop(0, total_c // WIN, carrier_block, 0)
    for t in range(2):
        for g in range(2):
            picked = mm(sel[...], kvc[t, g]).astype(BF16)
            for w in range(tiles):
                seen[t, g, w] = picked[w * SLOTS : (w + 1) * SLOTS]

    head_lane = lax.broadcasted_iota(jnp.int32, (1, 256), 1) // HEAD
    head_masks = [jnp.where(head_lane == h, 1.0, 0.0).astype(BF16) for h in range(4)]
    brow = lax.broadcasted_iota(jnp.int32, (128, 256), 0) // SLOTS
    bcol = lax.broadcasted_iota(jnp.int32, (128, 256), 1) // HEAD
    block_mask = jnp.where(brow == bcol, 1.0, 0.0).astype(BF16)
    slot_lane = lax.broadcasted_iota(jnp.int32, (1, 128), 1)
    slot_head = slot_lane // SLOTS
    slot_group = lax.rem(slot_lane, SLOTS) // PER_TILE

    def attend(w):
        bias = jnp.zeros((1, 128), F32)
        for c in range(1, SEEN):
            double = jnp.float32(0.0)
            for c2 in range(c):
                double = jnp.where(
                    adj[m * tiles + w, c] == adj[m * tiles + w, c2], jnp.float32(-1e30), double
                )
            bias = jnp.where(slot_group == c, double, bias)
        at = pl.ds(pl.multiple_of(w * WIN, WIN), WIN)
        for g in range(2):
            q = qkv[0, g, at]
            k = qkv[1, g, at]
            v = qkv[2, g, at]
            ks = jnp.concatenate([seen[0, g, w]] * 4, axis=0) * block_mask
            vs = jnp.concatenate([seen[1, g, w]] * 4, axis=0) * block_mask
            s_seen = mm_nt(q, ks) + bias
            top_seen = jnp.zeros((WIN, 128), F32)
            scs = [mm_nt(q * head_masks[h], k) for h in range(4)]
            prs = []
            for h in range(4):
                sc = scs[h]
                both = jnp.maximum(
                    jnp.maximum(sc[:, :128], sc[:, 128:]),
                    jnp.where(slot_head == h, s_seen, -jnp.inf),
                )
                top = jnp.max(both, axis=1, keepdims=True)
                prs.append(jnp.exp(sc - top).astype(BF16))
                top_seen = jnp.where(slot_head == h, top, top_seen)
            prs.append(jnp.exp(s_seen - top_seen).astype(BF16))
            pr = jnp.concatenate(prs, axis=1)
            vals = jnp.concatenate([v * head_masks[h] for h in range(4)] + [vs], axis=0)
            ones = jnp.concatenate(
                [jnp.broadcast_to(head_masks[h], (WIN, 256)) for h in range(4)] + [block_mask], axis=0
            )
            got = (mm(pr, vals) / mm(pr, ones)).astype(BF16)
            wout[pl.ds(pl.multiple_of((w + 1) * WIN, WIN), WIN), g * 256 : (g + 1) * 256] = got

    parts = []
    for g in range(2):
        qs = jnp.concatenate([qc[g]] * 4, axis=0) * block_mask
        sc = mm_nt(qs, kvc[0, g])
        pr = jnp.exp(sc - jnp.max(sc, axis=1, keepdims=True))
        low = pr.astype(BF16)
        res = mm(low, kvc[1, g]) / jnp.sum(pr, axis=1, keepdims=True)
        res = jnp.where(brow == bcol, res, 0.0)
        parts.append(res[0:32] + res[32:64] + res[64:96] + res[96:128])
    pull[pl.ds(rows, own_c), :] = jnp.concatenate(parts, axis=1).astype(BF16)

    attend(tiles - 1)
    out_halo = pltpu.make_async_remote_copy(
        src_ref=wout.at[pl.ds(tiles * WIN, WIN)],
        dst_ref=wout.at[pl.ds(0, WIN)],
        send_sem=os_sem,
        recv_sem=or_sem,
        device_id={"pix": far_pix, "mp": 1 - m},
        device_id_type=pl.DeviceIdType.MESH,
    )
    out_halo.start()

    def attend_one(w, _):
        attend(w)
        return 0

    lax.fori_loop(0, tiles - 1, attend_one, 0)

    wm_copy.wait()
    we_copy.wait()
    wc_copy.wait()
    sends[1].wait_recv()
    sends[2].wait_recv()
    sends[3].wait_recv()
    g2 = gain2[...]

    def finish(source, pulled):
        mid = (source.astype(F32) + (mm(pulled[:, :256], wm[0]) + mm(pulled[:, 256:], wm[1]))).astype(
            BF16
        )
        n2 = rms(mid, g2).astype(BF16)
        h0 = gelu(mm(n2, we[0])).astype(BF16)
        h1 = gelu(mm(n2, we[1])).astype(BF16)
        return (mid.astype(F32) + (mm(h0, wc[0]) + mm(h1, wc[1]))).astype(BF16)

    def out_copy(b):
        at = pl.ds(pl.multiple_of(b * WIN, WIN), WIN)
        return pltpu.make_async_copy(obuf.at[at], out_hbm.at[at], out_sem.at[b])

    def restore(b):
        at = pl.ds(pl.multiple_of(b * WIN, WIN), WIN)
        two = pl.ds(pl.multiple_of(b * WIN, WIN), 2 * WIN)
        pull[at, :] = mm(back, wout[two, :]).astype(BF16)

    def restore_one(b, _):
        restore(b)
        return 0

    lax.fori_loop(1, tiles, restore_one, 0)
    own_rows = cbuf[pl.ds(pl.multiple_of(p * own_c, own_c), own_c), :]
    done = finish(jnp.concatenate([xbuf[WIN:rows, :], own_rows], axis=0), pull[WIN:, :])
    obuf[WIN:, :] = done[: rows - WIN]
    outc[...] = done[rows - WIN :]

    def start_one(b, _):
        out_copy(b).start()
        return 0

    lax.fori_loop(1, tiles, start_one, 0)

    out_halo.wait()
    restore(0)
    obuf[0:WIN, :] = finish(xbuf[0:WIN, :], pull[0:WIN, :])
    out_copy(0).start()

    def out_wait(b, _):
        out_copy(b).wait()
        return 0

    lax.fori_loop(0, tiles, out_wait, 0)

    for i in range(4):
        sends[i].wait_send()

    def sent_carriers(k, _):
        carrier_copy(lax.rem(p + k, n), p).wait_send()
        return 0

    lax.fori_loop(1, n, sent_carriers, 0)

    @pl.when(m == 1)
    def _():
        halo_remote.wait_send()


def move(a_hbm, c_hbm, a_out, c_out, a_buf, c_buf, in_sem, out_sem):
    step = a_hbm.shape[0] // 4
    pairs = [
        (a_hbm.at[at], a_buf.at[at], a_out.at[at])
        for at in [pl.ds(i * step, step) for i in range(4)]
    ]
    pairs.append((c_hbm, c_buf, c_out))
    loads = [
        pltpu.make_async_copy(src, buf, in_sem.at[i]) for i, (src, buf, _) in enumerate(pairs)
    ]
    stores = [
        pltpu.make_async_copy(buf, dst, out_sem.at[i]) for i, (_, buf, dst) in enumerate(pairs)
    ]
    for copy in loads:
        copy.start()
    for load, store in zip(loads, stores):
        load.wait()
        store.start()
    for copy in stores:
        copy.wait()


def body(x, c, disp, labels, adj, gain1, gain2, wqkv, wm, we, wc):
    n = lax.axis_size("pix")
    rows = x.shape[0] // lax.axis_size("mp")
    tiles = rows // WIN
    width = x.shape[1]
    total_c = labels.shape[0]
    own_c = c.shape[0]
    vm = pl.BlockSpec(memory_space=pltpu.VMEM)
    sm = pl.BlockSpec(memory_space=pltpu.SMEM)
    hb = pl.BlockSpec(memory_space=pl.ANY)
    dma = pltpu.SemaphoreType.DMA
    results = pl.pallas_call(
        functools.partial(kernel, n),
        out_shape=(
            jax.ShapeDtypeStruct((rows, width), BF16),
            jax.ShapeDtypeStruct((own_c, width), BF16),
        ),
        in_specs=[hb, hb, sm, vm, sm, vm, vm, hb, hb, hb, hb],
        out_specs=(hb, vm),
        scratch_shapes=[
            pltpu.VMEM((rows + WIN, width), BF16),
            pltpu.VMEM((rows + WIN, width), BF16),
            pltpu.VMEM((3, 2, rows, 256), BF16),
            pltpu.VMEM((rows, width), BF16),
            pltpu.VMEM((rows + own_c, width), BF16),
            pltpu.VMEM((total_c, width), BF16),
            pltpu.VMEM((2, 2, total_c, 256), BF16),
            pltpu.VMEM((2, own_c, 256), BF16),
            pltpu.VMEM((tiles * SLOTS, total_c), BF16),
            pltpu.VMEM((2, 2, tiles, SLOTS, 256), BF16),
            pltpu.VMEM((rows + WIN, width), BF16),
            pltpu.VMEM((rows, width), BF16),
            pltpu.VMEM((2,) + wqkv.shape, BF16),
            pltpu.VMEM((2,) + wm.shape, BF16),
            pltpu.VMEM((2,) + we.shape, BF16),
            pltpu.VMEM((2,) + wc.shape, BF16),
            dma((7,)),
            dma((4,)),
            dma((4,)),
            dma,
            dma,
            dma((n,)),
            dma((n,)),
            dma,
            dma,
            dma((tiles,)),
        ],
        compiler_params=pltpu.CompilerParams(
            collective_id=0, has_side_effects=True, vmem_limit_bytes=58 * 1024 * 1024
        ),
    )(
        x,
        c,
        disp,
        labels.reshape(1, -1),
        adj,
        gain1.reshape(1, -1),
        gain2.reshape(1, -1),
        wqkv,
        wm,
        we,
        wc,
    )
    return pl.pallas_call(
        move,
        out_shape=[jax.ShapeDtypeStruct(r.shape, r.dtype) for r in results],
        in_specs=[hb, hb],
        out_specs=[hb, hb],
        scratch_shapes=[
            pltpu.VMEM((rows, width), BF16),
            pltpu.VMEM((own_c, width), BF16),
            dma((5,)),
            dma((5,)),
        ],
    )(*results)


def solution(mesh):
    return jax.shard_map(
        body,
        mesh=mesh,
        in_specs=(
            P(("groups", "pix"), None),
            P(("groups", "pix"), None),
            P(),
            P(),
            P("pix", None),
            P(),
            P(),
            P(None, None, "mp"),
            P("mp", None),
            P(None, "mp"),
            P("mp", None),
        ),
        out_specs=(P(("groups", "pix", "mp"), None), P(("groups", "pix"), None)),
        check_vma=False,
    )
```
